512 devices in a mesh: chan: 16 (over y, x_lo, core), slab: 32 (over z, x_hi).
Axes of the slice: x: 4 (x_hi: 2, x_lo: 2; x = x_hi * 2 + x_lo), y: 4, z: 16, core: 2. Of those that a mesh axis runs over, the one named last changes fastest.
Arguments:
- capture: bfloat16 [2, 2, 32, 3072, 2048], P(None, None, 'slab', 'chan'), may hold values from -6 to 6
- chirp_rates: float32 [2048], P('chan'), may hold values from 64 to 480
- phase_bin: int32 [98304], P('slab'), may hold values from 0 to 1023, as said below
- sub_id: int32 [98304], P('slab'), may hold values from 0 to 1, as said below
Outputs:
- folded: float32 [2048, 2, 1024], P(('chan', 'slab'))
The draws below stay inside these ranges and needn't reach their ends.
Inputs may be any that keep to these rules, and one draw needn't show every extreme that they name: phase_bin[t] = floor(1024 * frac((64 t + q) / m)) for an odd whole number m from 16384 to 65536 and a whole number q, both drawn with the window. `sub_id`: nondecreasing in time; it changes only between sample 98304 // 4 and sample 3 * 24576.
All inputs are finite; a program needn't handle non-finite values.
Results may differ from the reference program's by a relative error of at most 0.015.
Values may be sent and summed in bfloat16 or wider, within the bound.
No kernel may reach another device: no remote copies, remote signals or barrier semaphores. Data moves between devices by JAX's collectives and lax.ppermute only.
A program may use at most 64 MiB of HBM per device.

```python
import math
import jax
import jax.numpy as jnp
from jax import lax

CH = 2048
RADIX = 64
BINS = 1024
NSUB = 2
NFFT = 4096
NTAP = 1024
T_DEV = 3072
TIME = 98304
N_CHAN = 16
N_SLAB = 32


def draw_phase_bin(key, part):
    period = 2 * jax.random.randint(jax.random.fold_in(key, 11), (), 8 * BINS, 32 * BINS, dtype=jnp.int32) + 1
    offset = jax.random.randint(jax.random.fold_in(key, 12), (), 0, 16 * BINS, dtype=jnp.int32)
    sample = jnp.arange(TIME, dtype=jnp.int32)
    residue = (64 * sample + offset) % period
    return (residue * BINS // period).astype(jnp.int32)


def draw_sub_id(key, part):
    cut_points = jax.random.randint(jax.random.fold_in(key, 21), (NSUB - 1,), TIME // 4, 3 * TIME // 4 + 1, dtype=jnp.int32)
    sample = jnp.arange(TIME, dtype=jnp.int32)
    return jnp.sum((sample[:, None] >= cut_points[None, :]).astype(jnp.int32), axis=1).astype(jnp.int32)


def block_levels(own_key, extent, pieces, least, largest):
    loudness, own = 1.0, jax.random.fold_in(own_key, 6)
    for position, parts in pieces:
        heights = jnp.exp(jax.random.uniform(jax.random.fold_in(own, position), (parts,), jnp.float32, least / len(pieces), largest / len(pieces)))
        loudness = loudness * jnp.repeat(heights, extent[position] // parts).reshape([-1 if axis == position else 1 for axis in range(len(extent))])
    return loudness


def gaussian(key, extent, width, limit, split=(), kind=jnp.bfloat16):
    array = jax.random.normal(key, extent, jnp.float32) * width
    if len(split) > 0:
        array = block_levels(key, extent, split, -0.22, 0.18) * array
    return jnp.clip(array, min=-limit, max=limit).astype(kind)


def setup_inputs(seed: int = 0) -> dict:
    key_list = jax.random.split(jax.random.key(seed), 5)
    return {
        "capture": gaussian(key_list[0], (2, 2, N_SLAB, T_DEV, CH), 1.0, 6.0, ((2, 32), (3, 16))),
        "chirp_rates": jnp.clip(jnp.exp(math.log(480.0) - 2.014903 * jax.random.uniform(key_list[1], (CH,), jnp.float32) ** block_levels(key_list[1], (CH,), ((0, 16),), -0.2, 0.2)), 64.0, 480.0),
        "phase_bin": draw_phase_bin(jax.random.fold_in(key_list[4], 71), 0),
        "sub_id": draw_sub_id(jax.random.fold_in(key_list[4], 71), 0),
    }


def transform_tables():
    indices = jnp.arange(RADIX, dtype=jnp.int32)
    small = (indices[:, None] * indices[None, :]) % RADIX
    angles = (2.0 * math.pi / RADIX) * small.astype(jnp.float32)
    cosine = jnp.cos(angles)
    sine = jnp.sin(angles)
    forward = jnp.stack([jnp.stack([cosine, -sine], axis=1), jnp.stack([sine, cosine], axis=1)], axis=0).astype(jnp.bfloat16)
    inverse = jnp.stack([jnp.stack([cosine, sine], axis=1), jnp.stack([-sine, cosine], axis=1)], axis=0).astype(jnp.bfloat16)
    large = (indices[:, None] * indices[None, :]) % NFFT
    twist = (2.0 * math.pi / NFFT) * large.astype(jnp.float32)
    return forward, inverse, jnp.cos(twist)[:, :, None], jnp.sin(twist)[:, :, None]


def chirp_table(rates_here):
    indices = jnp.arange(RADIX, dtype=jnp.int32)
    spectral = indices[:, None] + RADIX * indices[None, :]
    offset = ((spectral + NFFT // 2) % NFFT).astype(jnp.float32) / NFFT
    turns = rates_here[None, None, :] * (offset * offset)[:, :, None]
    phase = (2.0 * math.pi) * (turns - jnp.floor(turns))
    return jnp.cos(phase), jnp.sin(phase)


def dedisperse(blocks, forward, inverse, twid_cos, twid_sin, chirp_cos, chirp_sin):
    high = lax.Precision.HIGHEST
    forward_wide = forward.astype(jnp.float32)
    inverse_wide = inverse.astype(jnp.float32)
    section_one = jnp.einsum('rask,xrabc->xskbc', forward_wide, blocks.astype(jnp.float32), precision=high)
    real_part, imag_part = section_one[:, 0], section_one[:, 1]
    middle = jnp.stack([real_part * twid_cos + imag_part * twid_sin, imag_part * twid_cos - real_part * twid_sin], axis=1).astype(jnp.bfloat16)
    spectrum = jnp.einsum('rbsw,xrkbc->xskwc', forward_wide, middle.astype(jnp.float32), precision=high)
    real_part, imag_part = spectrum[:, 0], spectrum[:, 1]
    filtered = jnp.stack([real_part * chirp_cos + imag_part * chirp_sin, imag_part * chirp_cos - real_part * chirp_sin], axis=1).astype(jnp.bfloat16)
    section_three = jnp.einsum('rwsa,xrkwc->xskac', inverse_wide, filtered.astype(jnp.float32), precision=high)
    real_part, imag_part = section_three[:, 0], section_three[:, 1]
    back = jnp.stack([real_part * twid_cos - imag_part * twid_sin, imag_part * twid_cos + real_part * twid_sin], axis=1).astype(jnp.bfloat16)
    section_four = jnp.einsum('rksb,xrkac->xsbac', inverse_wide, back.astype(jnp.float32), precision=high)
    kept = section_four[:, :, NTAP // RADIX:] * (1.0 / NFFT)
    voltage = kept.reshape(kept.shape[0], 2, -1, kept.shape[-1])
    return jnp.sum(voltage * voltage, axis=1)


def reference(capture, chirp_rates, phase_bin, sub_id):
    forward, inverse, twid_cos, twid_sin = transform_tables()
    slabs = capture.shape[2]
    span = capture.shape[3]
    total = slabs * span
    series = capture.reshape(2, 2, total, CH)
    padded = jnp.concatenate([jnp.zeros((2, 2, NTAP, CH), jnp.bfloat16), series], axis=2)
    starts = jnp.arange(slabs, dtype=jnp.int32) * span
    window = (starts[:, None] + jnp.arange(NFFT, dtype=jnp.int32)[None, :]).reshape(-1)
    group_width = CH // N_CHAN
    keys = (sub_id * BINS + phase_bin).astype(jnp.int32)
    scale = NSUB * BINS / (4.0 * total)

    def one_group(group):
        first = (group * group_width).astype(jnp.int32)
        chans = lax.dynamic_slice_in_dim(padded, first, group_width, axis=3)
        blocks = jnp.take(chans, window, axis=2).reshape(2, 2, slabs, NFFT, group_width)
        blocks = jnp.transpose(blocks, (2, 0, 1, 3, 4)).reshape(slabs * 2, 2, RADIX, RADIX, group_width)
        rates_here = lax.dynamic_slice_in_dim(chirp_rates, first, group_width)
        chirp_cos, chirp_sin = chirp_table(rates_here)
        detected = dedisperse(blocks, forward, inverse, twid_cos, twid_sin, chirp_cos, chirp_sin)
        detected = detected.reshape(slabs, 2, span, group_width)
        power = jnp.sum(detected, axis=1).astype(jnp.bfloat16).reshape(total, group_width)
        sums = jax.ops.segment_sum(power.astype(jnp.float32), keys, num_segments=NSUB * BINS)
        return sums.T.reshape(group_width, NSUB, BINS) * scale

    result = lax.map(one_group, jnp.arange(N_CHAN, dtype=jnp.int32))
    return result.reshape(CH, NSUB, BINS)
```

```python
import math

import jax
import jax.numpy as jnp
from jax import lax
from jax.sharding import PartitionSpec as P

RADIX = 64
BINS = 1024
NSUB = 2
NFFT = 4096
NTAP = 1024


def passed_along(shard, axis, by):
    length = lax.axis_size(axis)
    pairs = [(i, i + by) for i in range(length) if 0 <= i + by < length]
    return lax.ppermute(shard, axis, pairs)


def transform_tables():
    indices = jnp.arange(RADIX, dtype=jnp.int32)
    small = indices[:, None] * indices[None, :] % RADIX
    angles = 2.0 * math.pi / RADIX * small.astype(jnp.float32)
    cosine = jnp.cos(angles)
    sine = jnp.sin(angles)
    forward = jnp.stack(
        [jnp.stack([cosine, -sine], axis=1), jnp.stack([sine, cosine], axis=1)], axis=0
    ).astype(jnp.bfloat16)
    inverse = jnp.stack(
        [jnp.stack([cosine, sine], axis=1), jnp.stack([-sine, cosine], axis=1)], axis=0
    ).astype(jnp.bfloat16)
    large = indices[:, None] * indices[None, :] % NFFT
    twist = 2.0 * math.pi / NFFT * large.astype(jnp.float32)
    return (forward, inverse, jnp.cos(twist)[:, :, None], jnp.sin(twist)[:, :, None])


def chirp_table(rates_here):
    indices = jnp.arange(RADIX, dtype=jnp.int32)
    spectral = indices[:, None] + RADIX * indices[None, :]
    offset = ((spectral + NFFT // 2) % NFFT).astype(jnp.float32) / NFFT
    turns = rates_here[None, None, :] * (offset * offset)[:, :, None]
    phase = 2.0 * math.pi * (turns - jnp.floor(turns))
    return (jnp.cos(phase), jnp.sin(phase))


def detect_block(turned, tables):
    forward, inverse, twid_cos, twid_sin, chirp_cos, chirp_sin = tables
    pols = turned.shape[0]
    span = turned.shape[3]
    width = turned.shape[4]
    tail_rows = turned[:, :, :, span - NTAP :, :]
    previous = passed_along(tail_rows, "slab", 1)
    block_data = jnp.concatenate([previous, turned], axis=3).reshape(pols, 2, RADIX, RADIX, width)
    section_one = jnp.einsum(
        "rask,prabc->pskbc", forward, block_data, preferred_element_type=jnp.float32
    )
    real_part, imag_part = (section_one[:, 0], section_one[:, 1])
    middle = jnp.stack(
        [real_part * twid_cos + imag_part * twid_sin, imag_part * twid_cos - real_part * twid_sin],
        axis=1,
    ).astype(jnp.bfloat16)
    spectrum = jnp.einsum("rbsw,prkbc->pskwc", forward, middle, preferred_element_type=jnp.float32)
    real_part, imag_part = (spectrum[:, 0], spectrum[:, 1])
    filtered = jnp.stack(
        [
            real_part * chirp_cos + imag_part * chirp_sin,
            imag_part * chirp_cos - real_part * chirp_sin,
        ],
        axis=1,
    ).astype(jnp.bfloat16)
    section_three = jnp.einsum(
        "rwsa,prkwc->pskac", inverse, filtered, preferred_element_type=jnp.float32
    )
    real_part, imag_part = (section_three[:, 0], section_three[:, 1])
    back = jnp.stack(
        [real_part * twid_cos - imag_part * twid_sin, imag_part * twid_cos + real_part * twid_sin],
        axis=1,
    ).astype(jnp.bfloat16)
    section_four = jnp.einsum(
        "rksb,prkac->psbac", inverse, back, preferred_element_type=jnp.float32
    )
    kept = section_four[:, :, NTAP // RADIX :] * (1.0 / NFFT)
    voltage = kept.reshape(pols, 2, span, width)
    return jnp.sum(voltage * voltage, axis=1)


def shards(capture, chirp_rates, phase_bin, sub_id):
    forward, inverse, twid_cos, twid_sin = transform_tables()
    chirp_cos, chirp_sin = chirp_table(chirp_rates)
    tables = (forward, inverse, twid_cos, twid_sin, chirp_cos, chirp_sin)
    turned = lax.all_to_all(capture, "chan", split_axis=4, concat_axis=3, tiled=True)
    detected = detect_block(turned, tables)
    power = jnp.sum(detected, axis=0).astype(jnp.bfloat16)
    span = power.shape[0]
    onehot = (phase_bin[:, None] == jnp.arange(BINS, dtype=jnp.int32)[None, :]).astype(jnp.bfloat16)
    sub_masks = (sub_id[None, :] == jnp.arange(NSUB, dtype=jnp.int32)[:, None]).astype(jnp.bfloat16)
    weighted = sub_masks[:, :, None] * power[None, :, :]
    slab_count = lax.axis_size("slab")
    partial = jnp.einsum(
        "stc,tb->csb", weighted, onehot, preferred_element_type=jnp.float32
    ).astype(jnp.bfloat16)
    channels = partial.shape[0] // slab_count
    pieces = partial.reshape(slab_count, channels, NSUB, BINS)
    pieces = lax.all_to_all(pieces, "slab", split_axis=0, concat_axis=0, tiled=True)
    summed = jnp.sum(pieces.astype(jnp.float32), axis=0)
    scale = NSUB * BINS / (4.0 * span * slab_count)
    return summed * scale


def solution(mesh):
    placed = (P(None, None, "slab", "chan", None), P("chan"), P("slab"), P("slab"))
    return jax.shard_map(
        shards,
        mesh=mesh,
        in_specs=placed,
        out_specs=P(("chan", "slab"), None, None),
        check_vma=False,
    )
```

```python
import functools
import math

import jax
import jax.numpy as jnp
from jax import lax
from jax.experimental import pallas as pl
from jax.experimental.pallas import tpu as pltpu
from jax.sharding import Mesh
from jax.sharding import PartitionSpec as P

RADIX = 64
BINS = 1024
NSUB = 2
NFFT = 4096
NTAP = 1024
LANES = 128
GROUP = 32
QUADS = 4
PAGE = 256
KEYS = NSUB * BINS // PAGE
VMEM = pltpu.VMEM


def real_form(cosine, sine):
    top = jnp.concatenate([cosine, sine], axis=1)
    bottom = jnp.concatenate([-sine, cosine], axis=1)
    return jnp.concatenate([top, bottom], axis=0)


def transform_tables():
    indices = jnp.arange(RADIX, dtype=jnp.int32)
    small = indices[:, None] * indices[None, :] % RADIX
    angles = 2.0 * math.pi / RADIX * small.astype(jnp.float32)
    cosine = jnp.cos(angles).astype(jnp.bfloat16)
    sine = jnp.sin(angles).astype(jnp.bfloat16)
    forward = real_form(cosine, sine)
    inverse = real_form(cosine, -sine)
    first = NTAP // RADIX
    last = jnp.concatenate([inverse[first:RADIX], inverse[RADIX + first :]], axis=0)
    large = indices[:, None] * indices[None, :] % NFFT
    twist = 2.0 * math.pi / NFFT * large.astype(jnp.float32)
    shape = (RADIX, RADIX, LANES)
    twid_cos = jnp.broadcast_to(jnp.cos(twist)[:, :, None], shape).reshape(-1, LANES)
    twid_sin = jnp.broadcast_to(jnp.sin(twist)[:, :, None], shape).reshape(-1, LANES)
    return forward, inverse, last, twid_cos, twid_sin


def chirp_table(rates_here):
    indices = jnp.arange(RADIX, dtype=jnp.int32)
    spectral = indices[:, None] + RADIX * indices[None, :]
    offset = ((spectral + NFFT // 2) % NFFT).astype(jnp.float32) / NFFT
    turns = rates_here[None, None, :] * (offset * offset)[:, :, None]
    phase = 2.0 * math.pi * (turns - jnp.floor(turns))
    return jnp.cos(phase).reshape(-1, LANES), jnp.sin(phase).reshape(-1, LANES)


def iota(shape, axis):
    return lax.broadcasted_iota(jnp.int32, shape, axis)


def dot(a, b):
    return jnp.dot(a, b, preferred_element_type=jnp.float32)


def pack_kernel(groups, x_ref, o_ref, perm_ref):
    wide = 4 * LANES

    @pl.when(pl.program_id(0) == 0)
    def _():
        row, col = iota((wide, wide), 0), iota((wide, wide), 1)
        within = (row >> 4 & 7) * 4 + (row & 3)
        target = (row >> 2 & 3) * LANES + (row >> 7) * GROUP + within
        perm_ref[...] = jnp.where(col == target, 1.0, 0.0).astype(jnp.bfloat16)

    for g in range(groups):
        lanes = pl.ds(g * LANES, LANES)
        parts = [x_ref[p, r, 0, :, lanes] for p in range(2) for r in range(2)]
        out = dot(jnp.concatenate(parts, axis=1), perm_ref[...]).astype(jnp.bfloat16)
        for q in range(QUADS):
            o_ref[g * QUADS + q] = out[:, q * LANES : (q + 1) * LANES]


def pack(capture, groups=4):
    rows, channels = capture.shape[3:]
    chans = channels // LANES
    return pl.pallas_call(
        functools.partial(pack_kernel, groups),
        out_shape=jax.ShapeDtypeStruct((chans * QUADS, rows, LANES), jnp.bfloat16),
        grid=(chans // groups,),
        in_specs=[pl.BlockSpec((2, 2, 1, rows, groups * LANES), lambda g: (0, 0, 0, 0, g))],
        out_specs=pl.BlockSpec((groups * QUADS, rows, LANES), lambda g: (g, 0, 0)),
        scratch_shapes=[VMEM((4 * LANES, 4 * LANES), jnp.bfloat16)],
        name="pack",
    )(capture)


PITCH = 64


def detect_kernel(
    slabs, unroll, rx, halo, fwd, inv, last, tw_c, tw_s, ch_c, ch_s, o_ref, a_re, a_im, b_re, b_im
):
    sources, _, rows, _ = rx.shape
    wide = 2 * LANES
    row, col = iota((wide, wide), 0), iota((wide, wide), 1)
    target = (row >> 5 & 1) * LANES + (row >> 6 & 1) * 64 + (row >> 7) * GROUP + (row & 31)
    perm = jnp.where(col == target, 1.0, 0.0).astype(jnp.bfloat16)
    span = sources * rows
    tail = span - NTAP

    def unpack(pieces, start, size):
        both = dot(jnp.concatenate(pieces, axis=1), perm)
        a_re[pl.ds(start, size), :] = both[:, :LANES]
        a_im[pl.ds(start, size), :] = both[:, LANES:]

    for src in range(sources):
        unpack([rx[src, s] for s in slabs], NTAP + src * rows, rows)
        low = max(tail, src * rows)
        size = (src + 1) * rows - low
        if size > 0:
            pieces = []
            for s in slabs:
                if s == 0:
                    pieces.append(halo[low - tail : low - tail + size])
                else:
                    pieces.append(rx[src, s - 1, low - src * rows :])
            unpack(pieces, low - tail, size)

    def column(re, im, i):
        at = pl.ds(i, RADIX, stride=RADIX)
        return jnp.concatenate([re[at, :], im[at, :]], axis=0).astype(jnp.bfloat16)

    def block(re, im, i):
        at = pl.ds(pl.multiple_of(i * RADIX, RADIX), RADIX)
        return jnp.concatenate([re[at, :], im[at, :]], axis=0).astype(jnp.bfloat16)

    def split(out):
        half = out.shape[0] // 2
        return out[:half], out[half:]

    def at_of(i):
        return pl.ds(pl.multiple_of(i * RADIX, RADIX), RADIX)

    def first_stage(step, carry):
        for j in range(unroll):
            i = step * unroll + j
            re, im = split(dot(fwd[...], column(a_re, a_im, i)))
            cos, sin = tw_c[at_of(i), :], tw_s[at_of(i), :]
            b_re[at_of(i), :] = re * cos + im * sin
            b_im[at_of(i), :] = im * cos - re * sin
        return carry

    lax.fori_loop(0, RADIX // unroll, first_stage, 0)

    def middle_stages(step, carry):
        for j in range(unroll):
            i = step * unroll + j
            re, im = split(dot(fwd[...], column(b_re, b_im, i)))
            cos, sin = ch_c[at_of(i), :], ch_s[at_of(i), :]
            filtered = jnp.concatenate([re * cos + im * sin, im * cos - re * sin], axis=0)
            re, im = split(dot(inv[...], filtered.astype(jnp.bfloat16)))
            cos, sin = tw_c[at_of(i), :], tw_s[at_of(i), :]
            a_re[at_of(i), :] = re * cos - im * sin
            a_im[at_of(i), :] = im * cos + re * sin
        return carry

    lax.fori_loop(0, RADIX // unroll, middle_stages, 0)

    kept = last.shape[0] // 2

    def last_stage(step, carry):
        for j in range(unroll):
            i = step * unroll + j
            re, im = split(dot(last[...], column(a_re, a_im, i)) * (1.0 / NFFT))
            power = re * re + im * im
            power = power + pltpu.roll(power, 64, 1)
            o_ref[pl.ds(pl.multiple_of(i * kept, 16), kept), :] = power.astype(jnp.bfloat16)
        return carry

    lax.fori_loop(0, RADIX // unroll, last_stage, 0)


def detect(slabs, received, halo, tables, unroll=4):
    sources, _, rows, _ = received.shape
    span = sources * rows
    whole = pl.BlockSpec(memory_space=VMEM)
    args = [received, halo, *tables]
    flops = 2 * 2 * RADIX * 4 * 2 * RADIX * RADIX * LANES
    scratch = [VMEM((NFFT, LANES), jnp.float32)] * 4
    return pl.pallas_call(
        functools.partial(detect_kernel, slabs, unroll),
        out_shape=jax.ShapeDtypeStruct((span, LANES), jnp.bfloat16),
        in_specs=[whole] * len(args),
        out_specs=whole,
        scratch_shapes=scratch,
        cost_estimate=pl.CostEstimate(flops=flops, bytes_accessed=16 << 20, transcendentals=0),
        name="detect",
    )(*args)


def fold_kernel(late, early, keys, onehot, o_ref, turned):
    span = late.shape[0]
    chunk = 512
    lane = iota((LANES, LANES), 1)
    for t in range(span // LANES):
        at = pl.ds(t * LANES, LANES)
        both = jnp.where(lane < 64, early[at, :].astype(jnp.float32), late[at, :].astype(jnp.float32))
        turned[:, at] = both.T
    total = jnp.zeros((KEYS * GROUP, PAGE), jnp.float32)
    for q in range(QUADS):
        for t in range(span // chunk):
            at = pl.ds(t * chunk, chunk)
            own = turned[q * GROUP : (q + 1) * GROUP, at]
            key = jnp.broadcast_to(keys[q : q + 1, at], own.shape)
            picked = [jnp.where(key == u, own, 0.0).astype(jnp.bfloat16) for u in range(KEYS)]
            total = total + dot(jnp.concatenate(picked, axis=0), onehot[q, at, :])
    o_ref[...] = total.astype(jnp.bfloat16)


def fold(late, early, keys, onehot):
    whole = pl.BlockSpec(memory_space=VMEM)
    span = late.shape[0]
    flops = 2 * KEYS * GROUP * PAGE * QUADS * span
    return pl.pallas_call(
        fold_kernel,
        out_shape=jax.ShapeDtypeStruct((KEYS * GROUP, PAGE), jnp.bfloat16),
        in_specs=[whole] * 4,
        out_specs=whole,
        scratch_shapes=[VMEM((LANES, span), jnp.float32)],
        cost_estimate=pl.CostEstimate(flops=flops, bytes_accessed=8 << 20, transcendentals=0),
        name="fold",
    )(late, early, keys, onehot)


def swapped(x, axis):
    other = lax.ppermute(x, axis, [(0, 1), (1, 0)])
    low = lax.axis_index(axis) == 0
    return jnp.concatenate([jnp.where(low, x, other), jnp.where(low, other, x)], axis=0)


def shards(capture, chirp_rates, phase_bin, sub_id):
    rows = capture.shape[3]
    packed = pack(capture)
    received = lax.all_to_all(packed, ("chan", "zl", "xh"), 0, 0, tiled=True)
    received = received.reshape(-1, QUADS, rows, LANES)

    span = phase_bin.shape[0]
    keys = swapped(swapped((sub_id * BINS + phase_bin)[None], "xh"), "zl")
    keys = keys.reshape(QUADS, span // RADIX, RADIX).transpose(0, 2, 1).reshape(QUADS, span)
    own = lax.axis_index("zl") * 2 + lax.axis_index("xh")
    rates = lax.dynamic_index_in_dim(chirp_rates.reshape(-1, QUADS, 4), own, 1, False)
    rates = jnp.tile(rates.reshape(GROUP), LANES // GROUP)
    tables = (*transform_tables(), *chirp_table(rates))
    low = keys & (PAGE - 1)
    onehot = (low[:, :, None] == jnp.arange(PAGE, dtype=jnp.int32)).astype(jnp.bfloat16)

    tail = received[:, QUADS - 1].reshape(span, LANES)[span - NTAP :]
    blocks = lax.axis_size("zh")
    halo = lax.ppermute(tail, "zh", [(i, i + 1) for i in range(blocks - 1)])
    late = detect((2, 3), received, tail, tables)
    early = detect((0, 1), received, halo, tables)
    partial = fold(late, early, keys // PAGE, onehot)
    pieces = partial.reshape(KEYS, blocks, 4, PAGE).transpose(1, 0, 2, 3)
    pieces = lax.all_to_all(pieces.reshape(blocks, KEYS * 4, PAGE), "zh", 0, 0, tiled=True)
    scale = NSUB * BINS / (4.0 * span * blocks * QUADS)
    summed = jnp.sum(pieces.astype(jnp.float32), axis=0) * scale
    return summed.reshape(NSUB, BINS // PAGE, 4, PAGE).transpose(2, 0, 1, 3).reshape(4, NSUB, BINS)


def solution(mesh):
    chans, slabs = mesh.devices.shape
    fine = Mesh(mesh.devices.reshape(chans, slabs // QUADS, 2, 2), ("chan", "zh", "zl", "xh"))
    slab = ("zh", "zl", "xh")
    placed = (P(None, None, slab, "chan", None), P("chan"), P(slab), P(slab))
    return jax.shard_map(
        shards,
        mesh=fine,
        in_specs=placed,
        out_specs=P(("chan", *slab), None, None),
        check_vma=False,
    )
```

```python
import functools
import math

import jax
import jax.numpy as jnp
from jax import lax
from jax.experimental import pallas as pl
from jax.experimental.pallas import tpu as pltpu
from jax.sharding import Mesh
from jax.sharding import PartitionSpec as P

RADIX = 64
BINS = 1024
NSUB = 2
NFFT = 4096
NTAP = 1024
LANES = 128
GROUP = 32
QUADS = 4
PAGE = 256
KEYS = NSUB * BINS // PAGE
VMEM = pltpu.VMEM
GRANT = 16 << 20


def real_form(cosine, sine):
    top = jnp.concatenate([cosine, sine], axis=1)
    bottom = jnp.concatenate([-sine, cosine], axis=1)
    return jnp.concatenate([top, bottom], axis=0)


def transform_tables():
    indices = jnp.arange(RADIX, dtype=jnp.int32)
    small = indices[:, None] * indices[None, :] % RADIX
    angles = 2.0 * math.pi / RADIX * small.astype(jnp.float32)
    cosine = jnp.cos(angles).astype(jnp.bfloat16)
    sine = jnp.sin(angles).astype(jnp.bfloat16)
    forward = real_form(cosine, sine)
    inverse = real_form(cosine, -sine)
    first = NTAP // RADIX
    last = jnp.concatenate([inverse[first:RADIX], inverse[RADIX + first :]], axis=0)
    large = indices[:, None] * indices[None, :] % NFFT
    twist = 2.0 * math.pi / NFFT * large.astype(jnp.float32)
    row = jnp.arange(2 * LANES, dtype=jnp.int32)
    target = (row >> 5 & 1) * LANES + (row >> 6 & 1) * 64 + (row >> 7) * GROUP + (row & 31)
    perm = (target[:, None] == row[None, :]).astype(jnp.bfloat16)
    return (perm, forward, inverse, last), (jnp.cos(twist), jnp.sin(twist))


def chirp_table(rates_here):
    indices = jnp.arange(RADIX, dtype=jnp.int32)
    spectral = indices[:, None] + RADIX * indices[None, :]
    offset = ((spectral + NFFT // 2) % NFFT).astype(jnp.float32) / NFFT
    turns = rates_here[None, None, :] * (offset * offset)[:, :, None]
    phase = 2.0 * math.pi * (turns - jnp.floor(turns))
    return jnp.cos(phase).reshape(-1, LANES), jnp.sin(phase).reshape(-1, LANES)


def spread_kernel(tw_c, tw_s, ch_c, ch_s, otw_c, otw_s, och_c, och_s):
    for i in range(RADIX):
        at = pl.ds(i * RADIX, RADIX)
        otw_c[at, :] = jnp.broadcast_to(tw_c[:, i : i + 1], (RADIX, LANES))
        otw_s[at, :] = jnp.broadcast_to(tw_s[:, i : i + 1], (RADIX, LANES))
        och_c[at, :] = ch_c[at, :]
        och_s[at, :] = ch_s[at, :]


def all_tables(rates):
    matrices, twiddles = transform_tables()
    whole = pl.BlockSpec(memory_space=VMEM)
    spread = pl.pallas_call(
        spread_kernel,
        out_shape=[jax.ShapeDtypeStruct((NFFT, LANES), jnp.float32)] * 4,
        in_specs=[whole] * 4,
        out_specs=[whole] * 4,
        compiler_params=pltpu.CompilerParams(vmem_limit_bytes=GRANT),
        name="spread",
    )(*twiddles, *chirp_table(rates))
    return (*matrices, *spread)


def iota(shape, axis):
    return lax.broadcasted_iota(jnp.int32, shape, axis)


def dot(a, b):
    return jnp.dot(a, b, preferred_element_type=jnp.float32)


def pack_kernel(groups, x_ref, o_ref, perm_ref):
    wide = 4 * LANES

    @pl.when(pl.program_id(0) == 0)
    def _():
        row, col = iota((wide, wide), 0), iota((wide, wide), 1)
        within = (row >> 4 & 7) * 4 + (row & 3)
        target = (row >> 2 & 3) * LANES + (row >> 7) * GROUP + within
        perm_ref[...] = jnp.where(col == target, 1.0, 0.0).astype(jnp.bfloat16)

    for g in range(groups):
        lanes = pl.ds(g * LANES, LANES)
        parts = [x_ref[p, r, 0, :, lanes] for p in range(2) for r in range(2)]
        out = dot(jnp.concatenate(parts, axis=1), perm_ref[...]).astype(jnp.bfloat16)
        for q in range(QUADS):
            o_ref[g * QUADS + q] = out[:, q * LANES : (q + 1) * LANES]


def pack(capture, groups=4):
    rows, channels = capture.shape[3:]
    chans = channels // LANES
    return pl.pallas_call(
        functools.partial(pack_kernel, groups),
        out_shape=jax.ShapeDtypeStruct((chans * QUADS, rows, LANES), jnp.bfloat16),
        grid=(chans // groups,),
        in_specs=[pl.BlockSpec((2, 2, 1, rows, groups * LANES), lambda g: (0, 0, 0, 0, g))],
        out_specs=pl.BlockSpec((groups * QUADS, rows, LANES), lambda g: (g, 0, 0)),
        scratch_shapes=[VMEM((4 * LANES, 4 * LANES), jnp.bfloat16)],
        name="pack",
    )(capture)


PAIR = 2
PITCH = 68


def detect_kernel(
    slabs, unroll, rx, halo, perm, fwd, inv, last, tw_c, tw_s, ch_c, ch_s, o_ref, a_re, a_im, b_re, b_im
):
    sources, _, rows, _ = rx.shape
    span = sources * rows
    tail = span - NTAP

    def unpack(pieces, start, size):
        both = dot(jnp.concatenate(pieces, axis=1), perm[...])
        for j in range(size // RADIX):
            rows_at = pl.ds((start // RADIX + j) * PITCH, RADIX)
            part = both[j * RADIX : (j + 1) * RADIX]
            a_re[rows_at, :] = part[:, :LANES]
            a_im[rows_at, :] = part[:, LANES:]

    for src in range(sources):
        unpack([rx[src, s] for s in slabs], NTAP + src * rows, rows)
        low = max(tail, src * rows)
        size = (src + 1) * rows - low
        if size > 0:
            pieces = []
            for s in slabs:
                if s == 0:
                    pieces.append(halo[low - tail : low - tail + size])
                else:
                    pieces.append(rx[src, s - 1, low - src * rows :])
            unpack(pieces, low - tail, size)

    def column(re, im, i):
        at = pl.ds(i, RADIX, stride=PITCH)
        return jnp.concatenate([re[at, :], im[at, :]], axis=0).astype(jnp.bfloat16)

    def columns(re, im, i):
        return jnp.concatenate([column(re, im, i + j) for j in range(PAIR)], axis=1)

    def split(out, j):
        half = out.shape[0] // 2
        own = out[:, j * LANES : (j + 1) * LANES]
        return own[:half], own[half:]

    def at_of(i):
        return pl.ds(pl.multiple_of(i * RADIX, RADIX), RADIX)

    def pitched(i):
        return pl.ds(i * PITCH, RADIX)

    def loop(body):
        def many(step, carry):
            for j in range(unroll // PAIR):
                body(step * unroll + j * PAIR)
            return carry

        lax.fori_loop(0, RADIX // unroll, many, 0)

    def first_stage(i):
        out = dot(fwd[...], columns(a_re, a_im, i))
        for j in range(PAIR):
            re, im = split(out, j)
            cos, sin = tw_c[at_of(i + j), :], tw_s[at_of(i + j), :]
            b_re[pitched(i + j), :] = re * cos + im * sin
            b_im[pitched(i + j), :] = im * cos - re * sin

    loop(first_stage)

    def middle_stages(i):
        out = dot(fwd[...], columns(b_re, b_im, i))
        filtered = []
        for j in range(PAIR):
            re, im = split(out, j)
            cos, sin = ch_c[at_of(i + j), :], ch_s[at_of(i + j), :]
            both = jnp.concatenate([re * cos + im * sin, im * cos - re * sin], axis=0)
            filtered.append(both.astype(jnp.bfloat16))
        out = dot(inv[...], jnp.concatenate(filtered, axis=1))
        for j in range(PAIR):
            re, im = split(out, j)
            cos, sin = tw_c[at_of(i + j), :], tw_s[at_of(i + j), :]
            a_re[pitched(i + j), :] = re * cos - im * sin
            a_im[pitched(i + j), :] = im * cos + re * sin

    loop(middle_stages)

    kept = last.shape[0] // 2

    def last_stage(i):
        out = dot(last[...], columns(a_re, a_im, i)) * (1.0 / NFFT)
        for j in range(PAIR):
            re, im = split(out, j)
            power = re * re + im * im
            power = power + pltpu.roll(power, 64, 1)
            at = pl.ds(pl.multiple_of((i + j) * kept, 16), kept)
            o_ref[at, :] = power.astype(jnp.bfloat16)

    loop(last_stage)


def detect(slabs, received, halo, tables, unroll=32):
    sources, _, rows, _ = received.shape
    span = sources * rows
    whole = pl.BlockSpec(memory_space=VMEM)
    args = [received, halo, *tables]
    flops = 2 * 2 * RADIX * 4 * 2 * RADIX * RADIX * LANES
    scratch = [VMEM((RADIX * PITCH, LANES), jnp.float32)] * 4
    return pl.pallas_call(
        functools.partial(detect_kernel, slabs, unroll),
        out_shape=jax.ShapeDtypeStruct((span, LANES), jnp.bfloat16),
        in_specs=[whole] * len(args),
        out_specs=whole,
        scratch_shapes=scratch,
        cost_estimate=pl.CostEstimate(flops=flops, bytes_accessed=16 << 20, transcendentals=0),
        compiler_params=pltpu.CompilerParams(vmem_limit_bytes=GRANT),
        name="detect",
    )(*args)


def fold_kernel(late, early, keys, o_ref, turned):
    span = late.shape[0]
    chunk = 512
    lane = iota((LANES, LANES), 1)
    for t in range(span // LANES):
        at = pl.ds(t * LANES, LANES)
        both = jnp.where(lane < 64, early[at, :].astype(jnp.float32), late[at, :].astype(jnp.float32))
        turned[:, at] = both.T
    total = jnp.zeros((KEYS * GROUP, PAGE), jnp.float32)
    for q in range(QUADS):
        for t in range(span // chunk):
            at = pl.ds(t * chunk, chunk)
            code = keys[q : q + 1, at]
            shape = (KEYS, chunk)
            mine = jnp.broadcast_to(code >> 8, shape) == iota(shape, 0)
            picked = []
            for c in range(q * GROUP, (q + 1) * GROUP):
                own = jnp.broadcast_to(turned[c : c + 1, at], shape)
                picked.append(jnp.where(mine, own, 0.0))
            picked = jnp.concatenate(picked, axis=0).astype(jnp.bfloat16)
            low = jnp.broadcast_to(code & (PAGE - 1), (PAGE, chunk))
            onehot = jnp.where(low == iota((PAGE, chunk), 0), 1.0, 0.0).astype(jnp.bfloat16)
            total = total + lax.dot_general(
                picked,
                onehot,
                (((1,), (1,)), ((), ())),
                preferred_element_type=jnp.float32,
            )
    o_ref[...] = total.astype(jnp.bfloat16)


def fold(late, early, keys):
    whole = pl.BlockSpec(memory_space=VMEM)
    span = late.shape[0]
    flops = 2 * KEYS * GROUP * PAGE * QUADS * span
    return pl.pallas_call(
        fold_kernel,
        out_shape=jax.ShapeDtypeStruct((KEYS * GROUP, PAGE), jnp.bfloat16),
        in_specs=[whole] * 3,
        out_specs=whole,
        scratch_shapes=[VMEM((LANES, span), jnp.float32)],
        cost_estimate=pl.CostEstimate(flops=flops, bytes_accessed=8 << 20, transcendentals=0),
        compiler_params=pltpu.CompilerParams(vmem_limit_bytes=GRANT),
        name="fold",
    )(late, early, keys)


def shared(mine):
    across = [(0, 1), (1, 0)]
    both = [(0, 3), (1, 2), (2, 1), (3, 0)]
    by_x = lax.ppermute(mine, "xh", across)
    by_z = lax.ppermute(mine, "zl", across)
    by_both = lax.ppermute(mine, ("zl", "xh"), both)
    x_low, z_low = lax.axis_index("xh") == 0, lax.axis_index("zl") == 0
    near = jnp.concatenate([jnp.where(x_low, mine, by_x), jnp.where(x_low, by_x, mine)])
    far = jnp.concatenate([jnp.where(x_low, by_z, by_both), jnp.where(x_low, by_both, by_z)])
    return jnp.concatenate([jnp.where(z_low, near, far), jnp.where(z_low, far, near)])


def shards(capture, chirp_rates, phase_bin, sub_id):
    rows = capture.shape[3]
    packed = pack(capture)
    received = lax.all_to_all(packed, ("chan", "zl", "xh"), 0, 0, tiled=True)
    received = received.reshape(-1, QUADS, rows, LANES)

    span = phase_bin.shape[0]
    mine = (sub_id * BINS + phase_bin).reshape(span // RADIX, RADIX).T.reshape(1, span)
    keys = shared(mine)
    own = lax.axis_index("zl") * 2 + lax.axis_index("xh")
    rates = lax.dynamic_index_in_dim(chirp_rates.reshape(-1, QUADS, 4), own, 1, False)
    rates = jnp.tile(rates.reshape(GROUP), LANES // GROUP)
    tables = all_tables(rates)
    first = (span - NTAP) // rows
    tail = received[first:, QUADS - 1].reshape(-1, LANES)[-NTAP:]
    ready = jnp.maximum(tables[4][0, 0], tables[6][0, 0]) < 2.0
    tail = jnp.where(ready, tail, jnp.zeros_like(tail))
    blocks = lax.axis_size("zh")
    halo = lax.ppermute(tail, "zh", [(i, i + 1) for i in range(blocks - 1)])
    late = detect((2, 3), received, tail, tables)
    early = detect((0, 1), received, halo, tables)
    partial = fold(late, early, keys)
    pieces = partial.reshape(blocks, 4 * KEYS, PAGE)
    pieces = lax.all_to_all(pieces, "zh", 0, 0, tiled=True)
    scale = NSUB * BINS / (4.0 * span * blocks * QUADS)
    summed = jnp.sum(pieces.astype(jnp.float32), axis=0) * scale
    return summed.reshape(4, NSUB, BINS)


def solution(mesh):
    chans, slabs = mesh.devices.shape
    fine = Mesh(mesh.devices.reshape(chans, slabs // QUADS, 2, 2), ("chan", "zh", "zl", "xh"))
    slab = ("zh", "zl", "xh")
    placed = (P(None, None, slab, "chan", None), P("chan"), P(slab), P(slab))
    return jax.shard_map(
        shards,
        mesh=fine,
        in_specs=placed,
        out_specs=P(("chan", *slab), None, None),
        check_vma=False,
    )
```

```python
import functools
import math

import jax
import jax.numpy as jnp
from jax import lax
from jax.experimental import pallas as pl
from jax.experimental.pallas import tpu as pltpu
from jax.sharding import Mesh
from jax.sharding import PartitionSpec as P

RADIX = 64
BINS = 1024
NSUB = 2
NFFT = 4096
NTAP = 1024
LANES = 128
GROUP = 32
QUADS = 4
PAGE = 256
KEYS = NSUB * BINS // PAGE
VMEM = pltpu.VMEM
GRANT = 24 << 20
UNROLL = 32


def real_form(cosine, sine):
    top = jnp.concatenate([cosine, sine], axis=1)
    bottom = jnp.concatenate([-sine, cosine], axis=1)
    return jnp.concatenate([top, bottom], axis=0)


def transform_tables():
    indices = jnp.arange(RADIX, dtype=jnp.int32)
    small = indices[:, None] * indices[None, :] % RADIX
    angles = 2.0 * math.pi / RADIX * small.astype(jnp.float32)
    cosine = jnp.cos(angles).astype(jnp.bfloat16)
    sine = jnp.sin(angles).astype(jnp.bfloat16)
    forward = real_form(cosine, sine)
    inverse = real_form(cosine, -sine)
    first = NTAP // RADIX
    last = jnp.concatenate([inverse[first:RADIX], inverse[RADIX + first :]], axis=0)
    large = indices[:, None] * indices[None, :] % NFFT
    twist = 2.0 * math.pi / NFFT * large.astype(jnp.float32)
    shape = (RADIX, RADIX // UNROLL, UNROLL)
    twiddles = [w.reshape(shape).transpose(1, 0, 2) for w in (jnp.cos(twist), jnp.sin(twist))]
    return forward, inverse, last, *twiddles


def chirp_table(rates_here):
    indices = jnp.arange(RADIX, dtype=jnp.int32)
    spectral = indices[:, None] + RADIX * indices[None, :]
    offset = ((spectral + NFFT // 2) % NFFT).astype(jnp.float32) / NFFT
    turns = rates_here[None, None, :] * (offset * offset)[:, :, None]
    phase = 2.0 * math.pi * (turns - jnp.floor(turns))
    return jnp.cos(phase).reshape(-1, LANES), jnp.sin(phase).reshape(-1, LANES)


def iota(shape, axis):
    return lax.broadcasted_iota(jnp.int32, shape, axis)


def dot(a, b):
    return jnp.dot(a, b, preferred_element_type=jnp.float32)


def pack_kernel(groups, x_ref, o_ref):
    shape = (x_ref.shape[3], LANES)
    lane = iota(shape, 1)
    for g in range(groups):
        lanes = pl.ds(g * LANES, LANES)
        parts = [x_ref[p, r, 0, :, lanes] for p in range(2) for r in range(2)]
        for bit in range(2):
            step = 4 << bit
            low = (lane & step) == 0
            for s in range(4):
                if s & (1 << bit) == 0:
                    t = s | (1 << bit)
                    parts[s], parts[t] = (
                        jnp.where(low, parts[s], pltpu.roll(parts[t], step, 1)),
                        jnp.where(low, pltpu.roll(parts[s], LANES - step, 1), parts[t]),
                    )
        for q in range(QUADS):
            o_ref[g * QUADS + q] = parts[q]


def pack(capture, groups=4):
    rows, channels = capture.shape[3:]
    chans = channels // LANES
    return pl.pallas_call(
        functools.partial(pack_kernel, groups),
        out_shape=jax.ShapeDtypeStruct((chans * QUADS, rows, LANES), jnp.bfloat16),
        grid=(chans // groups,),
        in_specs=[pl.BlockSpec((2, 2, 1, rows, groups * LANES), lambda g: (0, 0, 0, 0, g))],
        out_specs=pl.BlockSpec((groups * QUADS, rows, LANES), lambda g: (g, 0, 0)),
        name="pack",
    )(capture)


PAIR = 2
PITCH = 68


def detect_kernel(
    slabs, rx, halo, fwd, inv, last, tw_c, tw_s, ch_c, ch_s, o_ref, a_re, a_im, b_re, b_im, c_c, c_s, sem
):
    chirps = [
        pltpu.make_async_copy(ch_c, c_c, sem.at[0]),
        pltpu.make_async_copy(ch_s, c_s, sem.at[1]),
    ]
    for copy in chirps:
        copy.start()
    unroll = UNROLL
    sources, _, rows, _ = rx.shape
    span = sources * rows
    tail = span - NTAP

    def unpack(pieces, start, size):
        one, two = pieces
        low = (iota(one.shape, 1) & 4) == 0
        re = jnp.where(low, one, pltpu.roll(two, 4, 1)).astype(jnp.float32)
        im = jnp.where(low, pltpu.roll(one, LANES - 4, 1), two).astype(jnp.float32)
        for j in range(size // RADIX):
            rows_at = pl.ds((start // RADIX + j) * PITCH, RADIX)
            a_re[rows_at, :] = re[j * RADIX : (j + 1) * RADIX]
            a_im[rows_at, :] = im[j * RADIX : (j + 1) * RADIX]

    for src in range(sources):
        unpack([rx[src, s] for s in slabs], NTAP + src * rows, rows)
        low = max(tail, src * rows)
        size = (src + 1) * rows - low
        if size > 0:
            pieces = []
            for s in slabs:
                if s == 0:
                    pieces.append(halo[low - tail : low - tail + size])
                else:
                    pieces.append(rx[src, s - 1, low - src * rows :])
            unpack(pieces, low - tail, size)

    def column(re, im, i):
        at = pl.ds(i, RADIX, stride=PITCH)
        return jnp.concatenate([re[at, :], im[at, :]], axis=0).astype(jnp.bfloat16)

    def columns(re, im, i):
        return jnp.concatenate([column(re, im, i + j) for j in range(PAIR)], axis=1)

    def split(out, j):
        half = out.shape[0] // 2
        own = out[:, j * LANES : (j + 1) * LANES]
        return own[:half], own[half:]

    def at_of(i):
        return pl.ds(pl.multiple_of(i * RADIX, RADIX), RADIX)

    def pitched(i):
        return pl.ds(i * PITCH, RADIX)

    def loop(body):
        def many(step, carry):
            for j in range(unroll // PAIR):
                body(step, j * PAIR)
            return carry

        lax.fori_loop(0, RADIX // unroll, many, 0)

    def twiddle(step, k):
        shape = (RADIX, LANES)
        return [jnp.broadcast_to(w[step, :, k : k + 1], shape) for w in (tw_c, tw_s)]

    def first_stage(step, k):
        i = step * unroll + k
        out = dot(fwd[...], columns(a_re, a_im, i))
        for j in range(PAIR):
            re, im = split(out, j)
            cos, sin = twiddle(step, k + j)
            b_re[pitched(i + j), :] = re * cos + im * sin
            b_im[pitched(i + j), :] = im * cos - re * sin

    loop(first_stage)
    for copy in chirps:
        copy.wait()

    def middle_stages(step, k):
        i = step * unroll + k
        out = dot(fwd[...], columns(b_re, b_im, i))
        filtered = []
        for j in range(PAIR):
            re, im = split(out, j)
            cos, sin = c_c[at_of(i + j), :], c_s[at_of(i + j), :]
            both = jnp.concatenate([re * cos + im * sin, im * cos - re * sin], axis=0)
            filtered.append(both.astype(jnp.bfloat16))
        out = dot(inv[...], jnp.concatenate(filtered, axis=1))
        for j in range(PAIR):
            re, im = split(out, j)
            cos, sin = twiddle(step, k + j)
            a_re[pitched(i + j), :] = re * cos - im * sin
            a_im[pitched(i + j), :] = im * cos + re * sin

    loop(middle_stages)

    kept = last.shape[0] // 2

    def last_stage(step, k):
        i = step * unroll + k
        out = dot(last[...], columns(a_re, a_im, i)) * (1.0 / NFFT)
        for j in range(PAIR):
            re, im = split(out, j)
            power = re * re + im * im
            power = power + pltpu.roll(power, LANES - 8 if slabs[0] == 0 else 8, 1)
            at = pl.ds(pl.multiple_of((i + j) * kept, 16), kept)
            o_ref[at, :] = power.astype(jnp.bfloat16)

    loop(last_stage)


def detect(slabs, received, halo, tables):
    sources, _, rows, _ = received.shape
    span = sources * rows
    whole = pl.BlockSpec(memory_space=VMEM)
    args = [received, halo, *tables]
    flops = 2 * 2 * RADIX * 4 * 2 * RADIX * RADIX * LANES
    scratch = [VMEM((RADIX * PITCH, LANES), jnp.float32)] * 4
    scratch += [VMEM((NFFT, LANES), jnp.float32)] * 2 + [pltpu.SemaphoreType.DMA((2,))]
    return pl.pallas_call(
        functools.partial(detect_kernel, slabs),
        out_shape=jax.ShapeDtypeStruct((span, LANES), jnp.bfloat16),
        in_specs=[whole] * (len(args) - 2) + [pl.BlockSpec(memory_space=pl.ANY)] * 2,
        out_specs=whole,
        scratch_shapes=scratch,
        cost_estimate=pl.CostEstimate(flops=flops, bytes_accessed=16 << 20, transcendentals=0),
        compiler_params=pltpu.CompilerParams(vmem_limit_bytes=GRANT),
        name="detect",
    )(*args)


def fold_kernel(late, early, keys, o_ref, turned):
    span = late.shape[0]
    chunk = 512
    lane = iota((LANES, LANES), 1)
    for t in range(span // LANES):
        at = pl.ds(t * LANES, LANES)
        both = jnp.where((lane & 8) == 0, early[at, :].astype(jnp.float32), late[at, :].astype(jnp.float32))
        turned[:, at] = both.T
    total = jnp.zeros((KEYS * GROUP, PAGE), jnp.float32)
    for q in range(QUADS):
        for t in range(span // chunk):
            at = pl.ds(t * chunk, chunk)
            code = keys[q : q + 1, at]
            shape = (KEYS, chunk)
            mine = jnp.broadcast_to(code >> 8, shape) == iota(shape, 0)
            picked = []
            for c in range(q * 4, LANES, 4 * QUADS):
                for i in range(c, c + 4):
                    own = jnp.broadcast_to(turned[i : i + 1, at], shape)
                    picked.append(jnp.where(mine, own, 0.0))
            picked = jnp.concatenate(picked, axis=0).astype(jnp.bfloat16)
            low = jnp.broadcast_to(code & (PAGE - 1), (PAGE, chunk))
            onehot = jnp.where(low == iota((PAGE, chunk), 0), 1.0, 0.0).astype(jnp.bfloat16)
            total = total + lax.dot_general(
                picked,
                onehot,
                (((1,), (1,)), ((), ())),
                preferred_element_type=jnp.float32,
            )
    o_ref[...] = total.astype(jnp.bfloat16)


def fold(late, early, keys):
    whole = pl.BlockSpec(memory_space=VMEM)
    span = late.shape[0]
    flops = 2 * KEYS * GROUP * PAGE * QUADS * span
    return pl.pallas_call(
        fold_kernel,
        out_shape=jax.ShapeDtypeStruct((KEYS * GROUP, PAGE), jnp.bfloat16),
        in_specs=[whole] * 3,
        out_specs=whole,
        scratch_shapes=[VMEM((LANES, span), jnp.float32)],
        cost_estimate=pl.CostEstimate(flops=flops, bytes_accessed=8 << 20, transcendentals=0),
        compiler_params=pltpu.CompilerParams(vmem_limit_bytes=GRANT),
        name="fold",
    )(late, early, keys)


def shared(mine):
    across = [(0, 1), (1, 0)]
    both = [(0, 3), (1, 2), (2, 1), (3, 0)]
    by_x = lax.ppermute(mine, "xh", across)
    by_z = lax.ppermute(mine, "zl", across)
    by_both = lax.ppermute(mine, ("zl", "xh"), both)
    x_low, z_low = lax.axis_index("xh") == 0, lax.axis_index("zl") == 0
    near = jnp.concatenate([jnp.where(x_low, mine, by_x), jnp.where(x_low, by_x, mine)])
    far = jnp.concatenate([jnp.where(x_low, by_z, by_both), jnp.where(x_low, by_both, by_z)])
    return jnp.concatenate([jnp.where(z_low, near, far), jnp.where(z_low, far, near)])


def shards(capture, chirp_rates, phase_bin, sub_id):
    rows = capture.shape[3]
    packed = pack(capture)
    received = lax.all_to_all(packed, ("chan", "zl", "xh"), 0, 0, tiled=True)
    received = received.reshape(-1, QUADS, rows, LANES)

    span = phase_bin.shape[0]
    mine = (sub_id * BINS + phase_bin).reshape(span // RADIX, RADIX).T.reshape(1, span)
    keys = shared(mine)
    own = lax.axis_index("zl") * 2 + lax.axis_index("xh")
    rates = lax.dynamic_index_in_dim(chirp_rates.reshape(-1, QUADS, 4), own, 1, False)
    rates = jnp.broadcast_to(rates[:, None, :], (GROUP // 4, 4, 4)).reshape(LANES)
    tables = (*transform_tables(), *chirp_table(rates))
    first = (span - NTAP) // rows
    tail = received[first:, QUADS - 1].reshape(-1, LANES)[-NTAP:]
    ready = tables[-1][0, 0] < 2.0
    tail = jnp.where(ready, tail, jnp.zeros_like(tail))
    blocks = lax.axis_size("zh")
    halo = lax.ppermute(tail, "zh", [(i, i + 1) for i in range(blocks - 1)])
    late = detect((2, 3), received, tail, tables)
    early = detect((0, 1), received, halo, tables)
    partial = fold(late, early, keys)
    pieces = partial.reshape(blocks, 4 * KEYS, PAGE)
    pieces = lax.all_to_all(pieces, "zh", 0, 0, tiled=True)
    scale = NSUB * BINS / (4.0 * span * blocks * QUADS)
    summed = jnp.sum(pieces.astype(jnp.float32), axis=0) * scale
    return summed.reshape(4, NSUB, BINS)


def solution(mesh):
    chans, slabs = mesh.devices.shape
    fine = Mesh(mesh.devices.reshape(chans, slabs // QUADS, 2, 2), ("chan", "zh", "zl", "xh"))
    slab = ("zh", "zl", "xh")
    placed = (P(None, None, slab, "chan", None), P("chan"), P(slab), P(slab))
    return jax.shard_map(
        shards,
        mesh=fine,
        in_specs=placed,
        out_specs=P(("chan", *slab), None, None),
        check_vma=False,
    )
```

```python
import functools
import math

import jax
import jax.numpy as jnp
import numpy as np
from jax import lax
from jax.experimental import pallas as pl
from jax.experimental.pallas import tpu as pltpu
from jax.sharding import Mesh
from jax.sharding import PartitionSpec as P

RADIX = 64
BINS = 1024
NSUB = 2
NFFT = 4096
NTAP = 1024
LANES = 128
GROUP = 32
QUADS = 4
PAGE = 256
KEYS = NSUB * BINS // PAGE
VMEM = pltpu.VMEM
GRANT = 20 << 20
UNROLL = 32


def real_form(cosine, sine):
    top = jnp.concatenate([cosine, sine], axis=1)
    bottom = jnp.concatenate([-sine, cosine], axis=1)
    return jnp.concatenate([top, bottom], axis=0)


def transform_tables():
    indices = jnp.arange(RADIX, dtype=jnp.int32)
    small = indices[:, None] * indices[None, :] % RADIX
    angles = 2.0 * math.pi / RADIX * small.astype(jnp.float32)
    cosine = jnp.cos(angles).astype(jnp.bfloat16)
    sine = jnp.sin(angles).astype(jnp.bfloat16)
    forward = real_form(cosine, sine)
    inverse = real_form(cosine, -sine)
    first = NTAP // RADIX
    last = jnp.concatenate([inverse[first:RADIX], inverse[RADIX + first :]], axis=0)
    large = indices[:, None] * indices[None, :] % NFFT
    twist = 2.0 * math.pi / NFFT * large.astype(jnp.float32)
    return (forward, inverse, last), (jnp.cos(twist), jnp.sin(twist))


def chirp_table(rates_here):
    indices = jnp.arange(RADIX, dtype=jnp.int32)
    spectral = indices[:, None] + RADIX * indices[None, :]
    offset = ((spectral + NFFT // 2) % NFFT).astype(jnp.float32) / NFFT
    turns = rates_here[None, None, :] * (offset * offset)[:, :, None]
    phase = 2.0 * math.pi * (turns - jnp.floor(turns))
    return jnp.cos(phase).reshape(-1, LANES), jnp.sin(phase).reshape(-1, LANES)


def spread_kernel(cos, sin, wide_cos, wide_sin):
    for i in range(RADIX):
        at = pl.ds(i * RADIX, RADIX)
        wide_cos[at, :] = jnp.broadcast_to(cos[:, i : i + 1], (RADIX, LANES))
        wide_sin[at, :] = jnp.broadcast_to(sin[:, i : i + 1], (RADIX, LANES))


def all_tables(rates):
    matrices, twiddles = transform_tables()
    whole = pl.BlockSpec(memory_space=VMEM)
    spread = pl.pallas_call(
        spread_kernel,
        out_shape=[jax.ShapeDtypeStruct((NFFT, LANES), jnp.float32)] * 2,
        in_specs=[whole] * 2,
        out_specs=[whole] * 2,
        compiler_params=pltpu.CompilerParams(vmem_limit_bytes=GRANT),
        name="spread",
    )(*twiddles)
    return (*matrices, *spread, *chirp_table(rates))


def iota(shape, axis):
    return lax.broadcasted_iota(jnp.int32, shape, axis)


def dot(a, b):
    return jnp.dot(a, b, preferred_element_type=jnp.float32)


def pack_kernel(groups, x_ref, perm_ref, o_ref):
    lane = iota((x_ref.shape[3], LANES), 1)
    for g in range(groups):
        lanes = pl.ds(g * LANES, LANES)
        parts = [x_ref[p, r, 0, :, lanes] for p in range(2) for r in range(2)]
        if g % 2 == 0:
            out = dot(jnp.concatenate(parts, axis=1), perm_ref[...]).astype(jnp.bfloat16)
            parts = [out[:, q * LANES : (q + 1) * LANES] for q in range(QUADS)]
        else:
            for bit in range(2):
                step = 4 << bit
                low = (lane & step) == 0
                for s in range(4):
                    if s & (1 << bit) == 0:
                        t = s | (1 << bit)
                        parts[s], parts[t] = (
                            jnp.where(low, parts[s], pltpu.roll(parts[t], step, 1)),
                            jnp.where(low, pltpu.roll(parts[s], LANES - step, 1), parts[t]),
                        )
        for q in range(QUADS):
            o_ref[g * QUADS + q] = parts[q]


def moved(target):
    row = np.arange(target.size)
    return jnp.asarray(target[:, None] == row[None, :], dtype=jnp.bfloat16)


def pack_moves():
    row = np.arange(QUADS * LANES)
    part, rest = row >> 7, row & 127
    return moved((rest >> 2 & 3) * LANES + (rest & 0x73) + part * 4)


def pack(capture, groups=8):
    rows, channels = capture.shape[3:]
    chans = channels // LANES
    wide = QUADS * LANES
    return pl.pallas_call(
        functools.partial(pack_kernel, groups),
        out_shape=jax.ShapeDtypeStruct((chans * QUADS, rows, LANES), jnp.bfloat16),
        grid=(chans // groups,),
        in_specs=[
            pl.BlockSpec((2, 2, 1, rows, groups * LANES), lambda g: (0, 0, 0, 0, g)),
            pl.BlockSpec((wide, wide), lambda g: (0, 0)),
        ],
        out_specs=pl.BlockSpec((groups * QUADS, rows, LANES), lambda g: (g, 0, 0)),
        name="pack",
    )(capture, pack_moves())


PAIR = 2
PITCH = 68


def detect_kernel(slabs, *refs):
    carried = None if slabs[0] > 0 else refs[0]
    rx, halo, keys, fwd, inv, last, tw_c, tw_s, ch_c, ch_s, o_ref = refs[-17:-6]
    a_re, a_im, b_re, b_im, powers, turned = refs[-6:]
    unroll = UNROLL
    sources, _, rows, _ = rx.shape
    span = sources * rows
    tail = span - NTAP

    def unpack(pieces, start, size):
        low = (iota((RADIX, LANES), 1) & 4) == 0
        for j in range(size // RADIX):
            rows_at = pl.ds((start // RADIX + j) * PITCH, RADIX)
            one, two = [piece(j * RADIX).astype(jnp.float32) for piece in pieces]
            a_re[rows_at, :] = jnp.where(low, one, pltpu.roll(two, 4, 1))
            a_im[rows_at, :] = jnp.where(low, pltpu.roll(one, LANES - 4, 1), two)

    def from_slab(src, s, first, j):
        return rx[src, s, pl.ds(first + j, RADIX), :]

    def from_halo(first, j):
        return halo[pl.ds(first + j, RADIX), :]

    partial = functools.partial
    for src in range(sources):
        unpack([partial(from_slab, src, s, 0) for s in slabs], NTAP + src * rows, rows)
        low = max(tail, src * rows)
        size = (src + 1) * rows - low
        if size > 0:
            skip = low - src * rows
            before = [
                partial(from_halo, low - tail) if s == 0 else partial(from_slab, src, s - 1, skip)
                for s in slabs
            ]
            unpack(before, low - tail, size)

    def column(re, im, i):
        at = pl.ds(i, RADIX, stride=PITCH)
        return jnp.concatenate([re[at, :], im[at, :]], axis=0).astype(jnp.bfloat16)

    def columns(re, im, i):
        return jnp.concatenate([column(re, im, i + j) for j in range(PAIR)], axis=1)

    def split(out, j):
        half = out.shape[0] // 2
        own = out[:, j * LANES : (j + 1) * LANES]
        return own[:half], own[half:]

    def at_of(i):
        return pl.ds(pl.multiple_of(i * RADIX, RADIX), RADIX)

    def pitched(i):
        return pl.ds(i * PITCH, RADIX)

    def loop(body):
        def many(step, carry):
            for j in range(unroll // PAIR):
                body(step, j * PAIR)
            return carry

        lax.fori_loop(0, RADIX // unroll, many, 0)

    def twiddle(i):
        return tw_c[at_of(i), :], tw_s[at_of(i), :]

    def first_stage(step, k):
        i = step * unroll + k
        out = dot(fwd[...], columns(a_re, a_im, i))
        for j in range(PAIR):
            re, im = split(out, j)
            cos, sin = twiddle(i + j)
            b_re[pitched(i + j), :] = re * cos + im * sin
            b_im[pitched(i + j), :] = im * cos - re * sin

    loop(first_stage)

    def middle_stages(step, k):
        i = step * unroll + k
        out = dot(fwd[...], columns(b_re, b_im, i))
        filtered = []
        for j in range(PAIR):
            re, im = split(out, j)
            cos, sin = ch_c[at_of(i + j), :], ch_s[at_of(i + j), :]
            both = jnp.concatenate([re * cos + im * sin, im * cos - re * sin], axis=0)
            filtered.append(both.astype(jnp.bfloat16))
        out = dot(inv[...], jnp.concatenate(filtered, axis=1))
        for j in range(PAIR):
            re, im = split(out, j)
            cos, sin = twiddle(i + j)
            a_re[pitched(i + j), :] = re * cos - im * sin
            a_im[pitched(i + j), :] = im * cos + re * sin

    loop(middle_stages)

    kept = last.shape[0] // 2

    def last_stage(step, k):
        i = step * unroll + k
        out = dot(last[...], columns(a_re, a_im, i)) * (1.0 / NFFT)
        for j in range(PAIR):
            re, im = split(out, j)
            power = re * re + im * im
            power = power + pltpu.roll(power, LANES - 8 if slabs[0] == 0 else 8, 1)
            at = pl.ds(pl.multiple_of((i + j) * kept, 16), kept)
            powers[at, :] = power.astype(jnp.bfloat16)

    loop(last_stage)

    for t in range(span // LANES):
        at = pl.ds(t * LANES, LANES)
        turned[:, at] = powers[at, :].astype(jnp.float32).T
    chunk = 512
    total = jnp.zeros((KEYS * GROUP, PAGE), jnp.float32) if carried is None else carried[...]
    for q in slabs:
        for t in range(span // chunk):
            at = pl.ds(t * chunk, chunk)
            code = keys[q : q + 1, at]
            shape = (KEYS, chunk)
            mine = jnp.broadcast_to(code >> 8, shape) == iota(shape, 0)
            picked = []
            for c in range(q * 4, LANES, 4 * QUADS):
                for i in range(c, c + 4):
                    own = jnp.broadcast_to(turned[i : i + 1, at], shape)
                    picked.append(jnp.where(mine, own, 0.0))
            picked = jnp.concatenate(picked, axis=0).astype(jnp.bfloat16)
            low = jnp.broadcast_to(code & (PAGE - 1), (PAGE, chunk))
            onehot = jnp.where(low == iota((PAGE, chunk), 0), 1.0, 0.0).astype(jnp.bfloat16)
            total = total + lax.dot_general(
                picked,
                onehot,
                (((1,), (1,)), ((), ())),
                preferred_element_type=jnp.float32,
            )
    o_ref[...] = total.astype(o_ref.dtype)


def detect(slabs, received, halo, keys, tables, carried=None):
    sources, _, rows, _ = received.shape
    span = sources * rows
    whole = pl.BlockSpec(memory_space=VMEM)
    args = [received, halo, keys, *tables]
    if carried is not None:
        args = [carried, *args]
    kind = jnp.float32 if carried is None else jnp.bfloat16
    flops = 2 * 2 * RADIX * 4 * 2 * RADIX * RADIX * LANES
    scratch = [VMEM((RADIX * PITCH, LANES), jnp.float32)] * 4
    scratch += [VMEM((span, LANES), jnp.bfloat16), VMEM((LANES, span), jnp.float32)]
    return pl.pallas_call(
        functools.partial(detect_kernel, slabs),
        out_shape=jax.ShapeDtypeStruct((KEYS * GROUP, PAGE), kind),
        in_specs=[whole] * len(args),
        out_specs=whole,
        scratch_shapes=scratch,
        cost_estimate=pl.CostEstimate(flops=flops, bytes_accessed=16 << 20, transcendentals=0),
        compiler_params=pltpu.CompilerParams(vmem_limit_bytes=GRANT),
        name="detect",
    )(*args)


def shared(mine):
    across = [(0, 1), (1, 0)]
    both = [(0, 3), (1, 2), (2, 1), (3, 0)]
    by_x = lax.ppermute(mine, "xh", across)
    by_z = lax.ppermute(mine, "zl", across)
    by_both = lax.ppermute(mine, ("zl", "xh"), both)
    x_low, z_low = lax.axis_index("xh") == 0, lax.axis_index("zl") == 0
    near = jnp.concatenate([jnp.where(x_low, mine, by_x), jnp.where(x_low, by_x, mine)])
    far = jnp.concatenate([jnp.where(x_low, by_z, by_both), jnp.where(x_low, by_both, by_z)])
    return jnp.concatenate([jnp.where(z_low, near, far), jnp.where(z_low, far, near)])


def shards(capture, chirp_rates, phase_bin, sub_id):
    rows = capture.shape[3]
    packed = pack(capture)
    received = lax.all_to_all(packed, ("chan", "zl", "xh"), 0, 0, tiled=True)
    received = received.reshape(-1, QUADS, rows, LANES)

    span = phase_bin.shape[0]
    mine = (sub_id * BINS + phase_bin).reshape(span // RADIX, RADIX).T.reshape(1, span)
    keys = shared(mine)
    own = lax.axis_index("zl") * 2 + lax.axis_index("xh")
    rates = lax.dynamic_index_in_dim(chirp_rates.reshape(-1, QUADS, 4), own, 1, False)
    rates = jnp.broadcast_to(rates[:, None, :], (GROUP // 4, 4, 4)).reshape(LANES)
    tables = all_tables(rates)
    first = (span - NTAP) // rows
    tail = received[first:, QUADS - 1].reshape(-1, LANES)[-NTAP:]
    ready = jnp.maximum(tables[3][0, 0], tables[5][0, 0]) < 2.0
    tail = jnp.where(ready, tail, jnp.zeros_like(tail))
    blocks = lax.axis_size("zh")
    halo = lax.ppermute(tail, "zh", [(i, i + 1) for i in range(blocks - 1)])
    late = detect((2, 3), received, tail, keys, tables)
    partial = detect((0, 1), received, halo, keys, tables, late)
    pieces = partial.reshape(blocks, 4 * KEYS, PAGE)
    pieces = lax.all_to_all(pieces, "zh", 0, 0, tiled=True)
    scale = NSUB * BINS / (4.0 * span * blocks * QUADS)
    summed = jnp.sum(pieces.astype(jnp.float32), axis=0) * scale
    return summed.reshape(4, NSUB, BINS)


def solution(mesh):
    chans, slabs = mesh.devices.shape
    fine = Mesh(mesh.devices.reshape(chans, slabs // QUADS, 2, 2), ("chan", "zh", "zl", "xh"))
    slab = ("zh", "zl", "xh")
    placed = (P(None, None, slab, "chan", None), P("chan"), P(slab), P(slab))
    return jax.shard_map(
        shards,
        mesh=fine,
        in_specs=placed,
        out_specs=P(("chan", *slab), None, None),
        check_vma=False,
    )
```
